768 devices in a mesh: ctx: 96 (over x, z, core), head: 8 (over y).
Axes of the slice: x: 4, y: 8, z: 12, core: 2. Of those that a mesh axis runs over, the one named last changes fastest.
Arguments:
- queries: bfloat16 [12288, 4096], P('ctx', 'head'), may hold values from -120 to 120
- keys: bfloat16 [12288, 1024], P('ctx', 'head'), may hold values from -4.5 to 4.5
- values: bfloat16 [12288, 1024], P('ctx', 'head'), may hold values from -6 to 6
- segments: int32 [12288], replicated, may hold values from 0 to 11, never falling along the last dimension, each value on 1 to 6144 neighbouring positions
- residual: bfloat16 [12288, 8192], P('ctx', 'head'), may hold values from -1.5 to 1.5
- out_weight: bfloat16 [4096, 8192], P('head'), may hold values from -1 to 1
Outputs:
- mixed: bfloat16 [12288, 8192], P('ctx', 'head')
The draws below stay inside these ranges and needn't reach their ends.
Inputs may be any that keep to these rules, and one draw needn't show every extreme that they name: `segments`: no document is longer than 6144 positions.
All inputs are finite; a program needn't handle non-finite values.
Results may differ from the reference program's by a relative error of at most 0.015.
Values may be sent and summed in bfloat16 or wider, within the bound.
No kernel may reach another device: no remote copies, remote signals or barrier semaphores. Data moves between devices by JAX's collectives and lax.ppermute only.
A program may use at most 128 MiB of HBM per device.

```python
import math
import jax
import jax.numpy as jnp
import numpy as np
from jax import lax

D = 8192
HD = 128
QH_DEV = 4
KV_HEADS = 8
Q_HEADS = 32
TOKENS = 12288
DOCMAX = 6144
N_CTX = 96


def paired_draw(key):
    key_seed = jax.random.fold_in(key, 101)
    query_seed = jax.random.fold_in(key, 202)
    key_rows = jnp.clip(jax.random.normal(key_seed, (TOKENS, KV_HEADS * HD), jnp.float32), -4.5, 4.5)
    query_rows = jnp.clip(2.5 * jax.random.normal(query_seed, (TOKENS, Q_HEADS * HD), jnp.float32), -15.0, 15.0)
    return (query_rows, key_rows)


def draw_queries(key, part):
    return paired_draw(key)[0].astype(jnp.bfloat16)


def draw_keys(key, part):
    return paired_draw(key)[1].astype(jnp.bfloat16)


def shard_levels(stream_key, dims, pieces, least, largest):
    gain = 1.0
    for dim, shards_of in pieces:
        draws = jax.random.uniform(jax.random.fold_in(jax.random.fold_in(stream_key, 6), dim), (shards_of,), jnp.float32, least / len(pieces), largest / len(pieces))
        gain = gain * jnp.repeat(jnp.exp(draws), dims[dim] // shards_of).reshape((-1,) + (1,) * (len(dims) - 1 - dim))
    return gain


def split_up(count, total, reach, slope):
    loads = [(1 << 20) // math.isqrt(standing ** slope) + 1 for standing in range(2, count + 1)]
    surplus, given = total - reach - (count - 1), [1] * (count - 1)
    while surplus > 0:
        movable = [i for i in range(count - 1) if given[i] < reach]
        mass, remaining = sum([loads[i] for i in movable]), surplus
        for i in movable:
            extra = min(reach - given[i], max(1, remaining * loads[i] // mass), surplus)
            given[i] = given[i] + extra
            surplus = surplus - extra
    return np.array([reach] + given)


def ragged(stream_key, amount, total, bound, slope):
    if amount == 2:
        one = jax.random.randint(stream_key, (), max(1, total - bound), min(bound, total - 1) + 1)
        return jnp.stack([one, total - one])
    sizes = jnp.asarray(split_up(amount, total, bound, slope), jnp.int32)
    twos = (amount - 1) // 2
    giver, sink = sizes[1:1 + 2 * twos:2], sizes[2:2 + 2 * twos:2]
    slack = jnp.minimum(giver - 1, bound - sink)
    moved = jax.random.randint(jax.random.fold_in(stream_key, 1), (twos,), 0, 1 << 20) % (slack + 1)
    sizes = sizes.at[1:1 + 2 * twos:2].set(giver - moved).at[2:2 + 2 * twos:2].set(sink + moved)
    return sizes[jax.random.permutation(jax.random.fold_in(stream_key, 2), amount)]


def gaussian(stream_key, dims, scale, reach, pieces=(), kind=jnp.bfloat16):
    loudness = shard_levels(stream_key, dims, pieces, -0.22, 0.18) if pieces else 1.0
    result = jax.random.normal(stream_key, dims, jnp.float32) * scale * loudness
    return jnp.minimum(jnp.maximum(result, -reach), reach).astype(kind)


def setup_inputs(seed: int = 0) -> dict:
    arg_keys = jax.random.split(jax.random.key(seed), 7)
    queries = draw_queries(jax.random.fold_in(arg_keys[6], 71), 0)
    keys = draw_keys(jax.random.fold_in(arg_keys[6], 71), 0)
    values = gaussian(arg_keys[2], (TOKENS, KV_HEADS * HD), 1.0, 6.0, ((0, 96), (1, 8)))
    segments = jnp.searchsorted(jnp.cumsum(ragged(arg_keys[3], max(3, N_CTX // 8), TOKENS, DOCMAX, 2)), jnp.arange(TOKENS), side="right").astype(jnp.int32)
    residual = gaussian(arg_keys[4], (TOKENS, D), 0.25, 1.5, ((0, 96), (1, 8)))
    out_weight = gaussian(arg_keys[5], (Q_HEADS * HD, D), Q_HEADS ** -0.5, 1.0, ((0, 8),))
    return dict(queries=queries, keys=keys, values=values, segments=segments, residual=residual, out_weight=out_weight)


def reference(queries, keys, values, segments, residual, out_weight):
    block_rows = math.gcd(512, TOKENS)
    key_span = min(TOKENS, DOCMAX + block_rows)
    score_scale = 1.0 / math.sqrt(HD)
    query_offsets = jnp.arange(block_rows, dtype=jnp.int32)
    key_offsets = jnp.arange(key_span, dtype=jnp.int32)

    def attend_block(block_index):
        query_first = (block_index * block_rows).astype(jnp.int32)
        key_first = jnp.clip(query_first + block_rows - key_span, 0, TOKENS - key_span).astype(jnp.int32)
        query_block = lax.dynamic_slice_in_dim(queries, query_first, block_rows, 0).astype(jnp.float32)
        query_block = query_block.reshape(block_rows, KV_HEADS, QH_DEV, HD)
        key_block = lax.dynamic_slice_in_dim(keys, key_first, key_span, 0).astype(jnp.float32)
        key_block = key_block.reshape(key_span, KV_HEADS, HD)
        value_block = lax.dynamic_slice_in_dim(values, key_first, key_span, 0).astype(jnp.float32)
        value_block = value_block.reshape(key_span, KV_HEADS, HD)
        query_segment = lax.dynamic_slice_in_dim(segments, query_first, block_rows, 0)
        key_segment = lax.dynamic_slice_in_dim(segments, key_first, key_span, 0)
        visible = (query_segment[:, None] == key_segment[None, :]) & ((key_first + key_offsets)[None, :] <= (query_first + query_offsets)[:, None])
        scores = jnp.einsum('qhgd,khd->hgqk', query_block, key_block) * score_scale
        scores = jnp.where(visible[None, None], scores, -jnp.inf)
        top_score = lax.optimization_barrier(jnp.max(scores, axis=-1, keepdims=True))
        raw_weights = jnp.exp(scores - top_score)
        total = lax.optimization_barrier(jnp.sum(raw_weights, axis=-1))
        weights = lax.optimization_barrier(raw_weights.astype(jnp.bfloat16)).astype(jnp.float32)
        summed = jnp.einsum('hgqk,khd->qhgd', weights, value_block)
        attended = summed / jnp.transpose(total, (2, 0, 1))[..., None]
        return attended.reshape(block_rows, Q_HEADS * HD).astype(jnp.bfloat16)
    attended = lax.map(attend_block, jnp.arange(TOKENS // block_rows, dtype=jnp.int32))
    attended = attended.reshape(TOKENS, Q_HEADS * HD)
    projected = jnp.dot(attended, out_weight, preferred_element_type=jnp.float32)
    return (residual.astype(jnp.float32) + projected).astype(jnp.bfloat16)
```

```python
import functools
import math

import jax
import jax.numpy as jnp
from jax import lax
from jax.experimental import pallas as pl
from jax.experimental.pallas import tpu as pltpu
from jax.sharding import Mesh, PartitionSpec as P

HD = 128
NX, NC = 4, 2
DOCS = 12
TILE = 256
LOW = -1e30
BF, F32 = jnp.bfloat16, jnp.float32


def nt(a, b):
    return lax.dot_general(a, b, (((1,), (1,)), ((), ())), preferred_element_type=F32)


def pack_kernel(k_ref, v_ref, kv_ref):
    kv_ref[:, :HD] = k_ref[...]
    kv_ref[:, HD:] = v_ref[...].astype(F32).T.astype(BF)


def split3(v):
    hi = v.astype(BF).astype(F32)
    mid = (v - hi).astype(BF).astype(F32)
    return hi, mid, v - hi - mid


def attend(steps, pos_ref, seg_ref, own_ref, other_ref, q_refs, out_refs, keys, vals, qrows, acc):
    nz = own_ref.shape[0] // HD
    rows = q_refs[0].shape[0]
    heads = q_refs[0].shape[1] // HD
    nq = heads * rows
    span = nz * NC * rows
    x, z, c = pos_ref[0], pos_ref[1], pos_ref[2]
    here = pos_ref[3]
    factor = math.log2(math.e) / math.sqrt(HD)

    def place(i, _):
        for ref, core in ((own_ref, c), (other_ref, 1 - c)):
            at = pl.multiple_of((i * NC + core) * rows, rows)
            src = pl.ds(pl.multiple_of(i * rows, rows), rows)
            keys[pl.ds(at, rows), :] = ref[src, :HD]
            vals[:, pl.ds(at, rows)] = ref[src, HD:]
        return 0

    lax.fori_loop(0, nz, place, 0)

    seg = seg_ref[...]
    below = [jnp.zeros((1, HD), F32)]
    for d in range(1, DOCS):
        below.append(jnp.sum((seg < d).astype(F32), axis=0, keepdims=True))
    below += [jnp.zeros((1, HD), F32)] * (16 - DOCS)
    below = jnp.sum(jnp.concatenate(below, axis=0), axis=1, keepdims=True).astype(jnp.int32)

    for n, s in enumerate(steps):
        exists = x + s < NX
        block = jnp.where(exists, here + s * nz * NC, here)
        seg_q = seg_ref[pl.ds(block, 1), :]
        first = jnp.zeros((1, rows), jnp.int32)
        for d in range(1, DOCS):
            first = jnp.where(seg_q >= d, below[d : d + 1, :], first)
        base = x * span
        lo = first - base
        hi0 = block * rows - base
        hi = hi0 + lax.broadcasted_iota(jnp.int32, (1, rows), 1)
        lo_min, lo_max = jnp.min(lo), jnp.max(lo)
        tiles = span // TILE
        a = jnp.clip(lo_min // TILE, 0, tiles)
        b = jnp.clip((hi0 + rows - 1) // TILE + 1, 0, tiles)
        a = jnp.where(exists, a, 0)
        b = jnp.where(exists, jnp.maximum(a, b), 0)
        full_a = jnp.clip((lo_max + TILE - 1) // TILE, a, b)
        full_b = jnp.clip((hi0 + 1) // TILE, full_a, b)
        lo_all = jnp.concatenate([lo] * heads, axis=1)
        width_all = jnp.concatenate([hi - lo] * heads, axis=1)

        for g in range(heads):
            qrows[g * rows : (g + 1) * rows, :] = q_refs[n][:, g * HD : (g + 1) * HD]
        acc[...] = jnp.zeros_like(acc)

        def body(masked, t, state):
            m, l = state
            at = pl.multiple_of(t * TILE, TILE)
            scores = nt(keys[pl.ds(at, TILE), :], qrows[...])
            if masked:
                off = lax.broadcasted_iota(jnp.int32, (TILE, nq), 0) + (at - lo_all)
                scores = jnp.where((off >= 0) & (off <= width_all), scores, -jnp.inf)
            m_new = jnp.maximum(m, jnp.max(scores, axis=0, keepdims=True))
            p = jnp.exp2((scores - m_new) * factor)
            fade = jnp.exp2((m - m_new) * factor)
            l = l * fade + jnp.sum(p, axis=0, keepdims=True)
            acc[...] = acc[...] * fade + jnp.dot(
                vals[:, pl.ds(at, TILE)], p.astype(BF), preferred_element_type=F32
            )
            return m_new, l

        state = (jnp.full((1, nq), LOW, F32), jnp.zeros((1, nq), F32))
        state = lax.fori_loop(a, full_a, functools.partial(body, True), state)
        state = lax.fori_loop(full_a, full_b, functools.partial(body, False), state)
        m, l = lax.fori_loop(full_b, b, functools.partial(body, True), state)

        if s == 0:
            o_ref, stat_ref = out_refs
            o_ref[...] = acc[...]
            stat_ref[0:1, :] = m
            stat_ref[1:2, :] = l
        else:
            out = out_refs[n]
            out[:HD, :] = acc[...].astype(BF)
            line = lax.broadcasted_iota(jnp.int32, (16, nq), 0)
            stat = jnp.zeros((16, nq), F32)
            for i, v in enumerate((*split3(m), *split3(l))):
                stat = jnp.where(line == i, v, stat)
            out[HD:, :] = stat.astype(BF)


def far_kernel(pos, seg, own, other, q1, q2, out1, out2, *scratch):
    attend((1, 2), pos, seg, own, other, (q1, q2), (out1, out2), *scratch)


def near_kernel(pos, seg, own, other, q, o, stat, *scratch):
    attend((0,), pos, seg, own, other, (q,), (o, stat), *scratch)


def merge_kernel(pos, o_ref, stat_ref, pay1, pay2, w_hbm, att_ref, r_ref, l_ref, w_vmem, sems):
    cols = r_ref.shape[1]
    rows = att_ref.shape[0]
    heads = att_ref.shape[1] // HD
    copies = []
    for i in range(2):
        at = pl.multiple_of(pos[4 + i] * cols, cols)
        copy = pltpu.make_async_copy(w_hbm.at[:, pl.ds(at, cols)], w_vmem.at[i], sems.at[i])
        copy.start()
        copies.append(copy)
    factor = math.log2(math.e) / math.sqrt(HD)
    parts = [(stat_ref[0:1, :], stat_ref[1:2, :], o_ref[...])]
    for s, pay in ((1, pay1), (2, pay2)):
        stat = pay[HD:, :].astype(F32)
        m = stat[0:1] + stat[1:2] + stat[2:3]
        l = stat[3:4] + stat[4:5] + stat[5:6]
        m = jnp.where(pos[0] >= s, m, LOW)
        parts.append((m, l, pay[:HD, :].astype(F32)))
    top = jnp.maximum(jnp.maximum(parts[0][0], parts[1][0]), parts[2][0])
    total, summed = 0.0, 0.0
    for m, l, o in parts:
        share = jnp.exp2((m - top) * factor)
        total = total + l * share
        summed = summed + o * share
    att = summed / total
    for g in range(heads):
        att_ref[:, g * HD : (g + 1) * HD] = att[:, g * rows : (g + 1) * rows].T.astype(BF)
    for i, out in enumerate((r_ref, l_ref)):
        copies[i].wait()
        out[...] = jnp.dot(att_ref[...], w_vmem[i], preferred_element_type=F32).astype(BF)


def project_kernel(idx, att_ref, w_ref, out_ref):
    out_ref[0] = jnp.dot(att_ref[...], w_ref[...], preferred_element_type=F32)


def vmem(n):
    return [pl.BlockSpec(memory_space=pltpu.VMEM)] * n


def local(queries, keys, values, segments, residual, out_weight):
    rows = queries.shape[0]
    heads = queries.shape[1] // HD
    nq = heads * rows
    nz, ny = lax.axis_size("z"), lax.axis_size("y")
    x, z, c, y = (lax.axis_index(n) for n in ("x", "z", "c", "y"))
    here = (x * nz + z) * NC + c
    cols = out_weight.shape[1] // ny
    half = ny // 2
    lane = jnp.arange(8, dtype=jnp.int32)
    pos = jnp.where(lane == 0, x, jnp.where(lane == 1, z, jnp.where(lane == 2, c, here)))
    pos = jnp.where(lane == 4, (y + half) % ny, jnp.where(lane == 5, (y + half + 1) % ny, pos))
    order = []
    for k in range(half - 1, 0, -1):
        order.append(k)
        if k > 1:
            order.append(-(k - 1))
    order.append(0)
    order = tuple(order)
    idx = (y + jnp.array(order, jnp.int32) + ny) % ny

    smem = pl.BlockSpec(memory_space=pltpu.SMEM)
    seg = segments.reshape(-1, HD)
    kv = pl.pallas_call(
        pack_kernel,
        out_shape=jax.ShapeDtypeStruct((rows, 2 * HD), BF),
        in_specs=vmem(2),
        out_specs=vmem(1)[0],
    )(keys, values)
    q1 = lax.ppermute(queries, "x", [(i + 1, i) for i in range(NX - 1)])
    q2 = lax.ppermute(queries, "x", [(i + 2, i) for i in range(NX - 2)])
    own = lax.all_gather(kv, "z", axis=0, tiled=True)
    other = lax.ppermute(own, "c", [(0, 1), (1, 0)])

    span = nz * NC * rows
    scratch = [
        pltpu.VMEM((span, HD), BF),
        pltpu.VMEM((HD, span), BF),
        pltpu.VMEM((nq, HD), BF),
        pltpu.VMEM((HD, nq), F32),
    ]
    work = 4 * nq * span * HD
    pay = jax.ShapeDtypeStruct((HD + 16, nq), BF)
    pay1, pay2 = pl.pallas_call(
        far_kernel,
        out_shape=(pay, pay),
        in_specs=[smem] + vmem(5),
        out_specs=tuple(vmem(2)),
        scratch_shapes=scratch,
        cost_estimate=pl.CostEstimate(flops=work, bytes_accessed=span * HD * 4, transcendentals=nq * span),
    )(pos, seg, own, other, q1, q2)
    back1 = lax.ppermute(pay1, "x", [(i, i + 1) for i in range(NX - 1)])
    back2 = lax.ppermute(pay2, "x", [(i, i + 2) for i in range(NX - 2)])
    o, stat = pl.pallas_call(
        near_kernel,
        out_shape=(jax.ShapeDtypeStruct((HD, nq), F32), jax.ShapeDtypeStruct((8, nq), F32)),
        in_specs=[smem] + vmem(4),
        out_specs=tuple(vmem(2)),
        scratch_shapes=scratch,
        cost_estimate=pl.CostEstimate(flops=work, bytes_accessed=span * HD * 4, transcendentals=nq * span),
    )(pos, seg, own, other, queries)

    piece = jax.ShapeDtypeStruct((rows, cols), BF)
    att, right, left = pl.pallas_call(
        merge_kernel,
        out_shape=(jax.ShapeDtypeStruct((rows, heads * HD), BF), piece, piece),
        in_specs=[smem] + vmem(4) + [pl.BlockSpec(memory_space=pl.ANY)],
        out_specs=tuple(vmem(3)),
        scratch_shapes=[pltpu.VMEM((2, heads * HD, cols), BF), pltpu.SemaphoreType.DMA((2,))],
    )(pos, o, stat, back1, back2, out_weight)
    parts = pl.pallas_call(
        project_kernel,
        out_shape=jax.ShapeDtypeStruct((len(order), rows, cols), F32),
        grid_spec=pltpu.PrefetchScalarGridSpec(
            num_scalar_prefetch=1,
            grid=(len(order),),
            in_specs=[
                pl.BlockSpec((rows, heads * HD), lambda i, idx: (0, 0)),
                pl.BlockSpec((heads * HD, cols), lambda i, idx: (0, idx[i])),
            ],
            out_specs=pl.BlockSpec((1, rows, cols), lambda i, idx: (i, 0, 0)),
        ),
        cost_estimate=pl.CostEstimate(
            flops=2 * rows * heads * HD * cols * len(order),
            bytes_accessed=len(order) * cols * heads * HD * 2,
            transcendentals=0,
        ),
    )(idx, att, out_weight)
    part = {k: parts[i] for i, k in enumerate(order)}

    up = [(i, (i + 1) % ny) for i in range(ny)]
    down = [(i, (i - 1) % ny) for i in range(ny)]
    for k in range(half - 1, -1, -1):
        right = lax.ppermute(right, "y", up).astype(F32)
        if k:
            right = (right + part[k]).astype(BF)
    for k in range(half - 2, -1, -1):
        left = lax.ppermute(left, "y", down).astype(F32)
        if k:
            left = (left + part[-k]).astype(BF)
    return (residual.astype(F32) + part[0] + right + left).astype(BF)


def solution(mesh):
    devices = mesh.devices
    ctx, ny = devices.shape
    fine = Mesh(devices.reshape(NX, ctx // (NX * NC), NC, ny), ("x", "z", "c", "y"))
    tok = ("x", "z", "c")
    placed = (P(tok, "y"), P(tok, "y"), P(tok, "y"), P(), P(tok, "y"), P("y", None))
    return jax.shard_map(
        local, mesh=fine, in_specs=placed, out_specs=P(tok, "y"), check_vma=False
    )
```

```python
import functools
import math

import jax
import jax.numpy as jnp
from jax import lax
from jax.experimental import pallas as pl
from jax.experimental.pallas import tpu as pltpu
from jax.sharding import Mesh, PartitionSpec as P

HD = 128
NX, NC = 4, 2
DOCS = 12
LOW = -1e30
FACTOR = math.log2(math.e) / math.sqrt(HD)
BF, F32 = jnp.bfloat16, jnp.float32
VMEM_BYTES = 24 << 20


def nt(a, b):
    return lax.dot_general(a, b, (((1,), (1,)), ((), ())), preferred_element_type=F32)


def dot(a, b):
    return jnp.dot(a, b, preferred_element_type=F32)


def pack_kernel(k_ref, v_ref, kv_ref):
    kv_ref[:, :HD] = k_ref[...]
    kv_ref[:, HD:] = v_ref[...].astype(F32).T.astype(BF)


def split3(v):
    hi = v.astype(BF).astype(F32)
    mid = (v - hi).astype(BF).astype(F32)
    return hi, mid, v - hi - mid


def attend(steps, seg_ref, own_ref, other_ref, q_refs, out_refs, acc, bias):
    nz = own_ref.shape[0] // HD
    rows = q_refs[0].shape[0]
    heads = q_refs[0].shape[1] // HD
    tile = NC * rows
    x, z, c = (lax.axis_index(n) for n in ("x", "z", "c"))
    here = (x * nz + z) * NC + c

    seg = seg_ref[...]
    below = [jnp.zeros((1, HD), F32)]
    for d in range(1, DOCS):
        below.append(jnp.sum((seg < d).astype(F32), axis=0, keepdims=True))
    below += [jnp.zeros((1, HD), F32)] * (16 - DOCS)
    below = jnp.sum(jnp.concatenate(below, axis=0), axis=1, keepdims=True).astype(jnp.int32)

    for n, s in enumerate(steps):
        exists = x + s < NX
        block = jnp.where(exists, here + s * nz * NC, here)
        seg_q = seg_ref[pl.ds(block, 1), :]
        first = jnp.zeros((1, rows), jnp.int32)
        for d in range(1, DOCS):
            first = jnp.where(seg_q >= d, below[d : d + 1, :], first)
        base = x * nz * tile
        lo = first - base
        hi0 = block * rows - base
        width = hi0 + lax.broadcasted_iota(jnp.int32, (1, rows), 1) - lo
        lo_min, lo_max = jnp.min(lo), jnp.max(lo)
        a = jnp.clip(lo_min // tile, 0, nz)
        b = jnp.clip((hi0 + rows - 1) // tile + 1, 0, nz)
        a = jnp.where(exists, a, 0)
        b = jnp.where(exists, jnp.maximum(a, b), 0)
        full_a = jnp.clip((lo_max + tile - 1) // tile, a, b)
        full_b = jnp.clip((hi0 + 1) // tile, full_a, b)
        acc[...] = jnp.zeros_like(acc)

        def body(masked, t, state):
            src = pl.ds(pl.multiple_of(t * rows, rows), rows)
            if masked:
                for i, core in enumerate((c, 1 - c)):
                    at = (t * NC + core) * rows
                    off = lax.broadcasted_iota(jnp.int32, (rows, rows), 0) + (at - lo)
                    seen = (off >= 0) & (off <= width)
                    bias[i] = jnp.where(seen, 0.0, -jnp.inf)
            new = []
            for g in range(heads):
                m, l = state[g]
                at = slice(g * HD, (g + 1) * HD)
                q = q_refs[n][:, at]
                scores = [nt(ref[src, :HD], q) for ref in (own_ref, other_ref)]
                if masked:
                    scores = [v + bias[i] for i, v in enumerate(scores)]
                top = jnp.max(jnp.maximum(scores[0], scores[1]), axis=0, keepdims=True)
                m_new = jnp.maximum(m, top)
                fade = jnp.exp2((m - m_new) * FACTOR)
                p = [jnp.exp2((v - m_new) * FACTOR) for v in scores]
                l = l * fade + jnp.sum(p[0] + p[1], axis=0, keepdims=True)
                summed = acc[:, at] * fade
                for ref, v in zip((own_ref, other_ref), p):
                    summed = summed + dot(ref[src, HD:], v.astype(BF))
                acc[:, at] = summed
                new.append((m_new, l))
            return tuple(new)

        state = ((jnp.full((1, rows), LOW, F32), jnp.zeros((1, rows), F32)),) * heads
        state = lax.fori_loop(a, full_a, functools.partial(body, True), state)
        state = lax.fori_loop(full_a, full_b, functools.partial(body, False), state)
        state = lax.fori_loop(full_b, b, functools.partial(body, True), state)

        for g in range(heads):
            m, l = state[g]
            at = slice(g * HD, (g + 1) * HD)
            if s == 0:
                o_ref, stat_ref = out_refs
                o_ref[:, at] = acc[:, at]
                stat_ref[0:1, at] = m
                stat_ref[1:2, at] = l
            else:
                out = out_refs[n]
                out[:HD, at] = acc[:, at].astype(BF)
                line = lax.broadcasted_iota(jnp.int32, (16, rows), 0)
                stat = jnp.zeros((16, rows), F32)
                for i, v in enumerate((*split3(m), *split3(l))):
                    stat = jnp.where(line == i, v, stat)
                out[HD:, at] = stat.astype(BF)


def far_kernel(seg, own, other, q1, q2, out1, out2, *scratch):
    attend((1, 2), seg, own, other, (q1, q2), (out1, out2), *scratch)


def near_kernel(seg, own, other, q, o, stat, *scratch):
    attend((0,), seg, own, other, (q,), (o, stat), *scratch)


def fetch(w_hbm, w_vmem, sems, dests):
    cols = w_vmem.shape[2]
    copies = []
    for i, dest in enumerate(dests):
        at = pl.multiple_of(dest * cols, cols)
        copy = pltpu.make_async_copy(w_hbm.at[:, pl.ds(at, cols)], w_vmem.at[i], sems.at[i])
        copy.start()
        copies.append(copy)
    return copies


def ahead(k):
    ny = lax.axis_size("y")
    return lax.rem(lax.axis_index("y") + k * (1 - 2 * lax.axis_index("c")) + ny, ny)


def merge_kernel(o_ref, stat_ref, pay1, pay2, w_hbm, att_ref, p_ref, w_vmem, sems):
    heads = att_ref.shape[1] // HD
    (copy,) = fetch(w_hbm, w_vmem, sems, (ahead(lax.axis_size("y") // 2),))
    x = lax.axis_index("x")
    for g in range(heads):
        at = slice(g * HD, (g + 1) * HD)
        parts = [(stat_ref[0:1, at], stat_ref[1:2, at], o_ref[:, at])]
        for s, pay in ((1, pay1), (2, pay2)):
            stat = pay[HD:, at].astype(F32)
            m = stat[0:1] + stat[1:2] + stat[2:3]
            l = stat[3:4] + stat[4:5] + stat[5:6]
            parts.append((jnp.where(x >= s, m, LOW), l, pay[:HD, at].astype(F32)))
        top = jnp.maximum(jnp.maximum(parts[0][0], parts[1][0]), parts[2][0])
        total, summed = 0.0, 0.0
        for m, l, o in parts:
            share = jnp.exp2((m - top) * FACTOR)
            total = total + l * share
            summed = summed + o * share
        att_ref[:, at] = (summed / total).T.astype(BF)
    copy.wait()
    p_ref[...] = dot(att_ref[...], w_vmem[0]).astype(BF)


def first_kernel(att, att_other, w_hbm, q_ref, p_ref, w_vmem, sems):
    (copy,) = fetch(w_hbm, w_vmem, sems, (ahead(lax.axis_size("y") // 2 - 1),))
    copy.wait()
    q_ref[...] = dot(att_other[...], w_vmem[0]).astype(BF)
    p_ref[...] = dot(att[...], w_vmem[0])


def rest_kernel(att, att_other, w_hbm, *refs):
    outs, (w_vmem, sems) = refs[:-2], refs[-2:]
    n = w_vmem.shape[0]
    copies = fetch(w_hbm, w_vmem, sems, [ahead(n - 1 - i) for i in range(n)])
    for i in range(n):
        copies[i].wait()
        outs[2 * i][...] = dot(att[...], w_vmem[i])
        if i < n - 1:
            outs[2 * i + 1][...] = dot(att_other[...], w_vmem[i])


def vmem(n):
    return [pl.BlockSpec(memory_space=pltpu.VMEM)] * n


def call(kernel, out_shape, args, hbm=None, scratch=(), cost=None):
    args = [pltpu.with_memory_space_constraint(a, pltpu.VMEM) for a in args]
    specs = vmem(len(args))
    if hbm is not None:
        args.append(hbm)
        specs.append(pl.BlockSpec(memory_space=pl.ANY))
    return pl.pallas_call(
        kernel,
        out_shape=tuple(out_shape),
        in_specs=specs,
        out_specs=tuple(vmem(len(out_shape))),
        scratch_shapes=list(scratch),
        cost_estimate=cost,
        compiler_params=pltpu.CompilerParams(vmem_limit_bytes=VMEM_BYTES),
    )(*args)


def local(queries, keys, values, segments, residual, out_weight):
    rows = queries.shape[0]
    width = queries.shape[1]
    nq = width // HD * rows
    nz, ny = lax.axis_size("z"), lax.axis_size("y")
    cols = out_weight.shape[1] // ny
    half = ny // 2
    sds = jax.ShapeDtypeStruct
    seg = segments.reshape(-1, HD)

    q1 = lax.ppermute(queries, "x", [(i + 1, i) for i in range(NX - 1)])
    q2 = lax.ppermute(queries, "x", [(i + 2, i) for i in range(NX - 2)])
    (kv,) = call(pack_kernel, [sds((rows, 2 * HD), BF)], (keys, values))
    own = lax.all_gather(kv, "z", axis=0, tiled=True)
    other = lax.ppermute(own, "c", [(0, 1), (1, 0)])

    scratch = [pltpu.VMEM((HD, nq), F32), pltpu.VMEM((2, rows, rows), F32)]
    work = 4 * nq * nz * NC * rows * HD // 2
    cost = pl.CostEstimate(flops=work, bytes_accessed=nz * rows * HD * 8, transcendentals=work // 512)
    pay = sds((HD + 16, nq), BF)
    pay1, pay2 = call(far_kernel, [pay, pay], (seg, own, other, q1, q2), None, scratch, cost)
    back1 = lax.ppermute(pay1, "x", [(i, i + 1) for i in range(NX - 1)])
    back2 = lax.ppermute(pay2, "x", [(i, i + 2) for i in range(NX - 2)])
    o, stat = call(
        near_kernel, [sds((HD, nq), F32), sds((8, nq), F32)], (seg, own, other, queries), None, scratch, cost
    )

    def weights(n):
        return [pltpu.VMEM((n, width, cols), BF), pltpu.SemaphoreType.DMA((n,))]

    def mat(n):
        return pl.CostEstimate(
            flops=2 * n * rows * width * cols, bytes_accessed=n * cols * width, transcendentals=0
        )

    sent, kept = sds((rows, cols), BF), sds((rows, cols), F32)
    att, mine = call(
        merge_kernel, [sds((rows, width), BF), sent], (o, stat, back1, back2), out_weight, weights(1), mat(1)
    )
    ring = [(i, (i + 1) % ny) for i in range(ny)] + [(ny + i, ny + (i - 1) % ny) for i in range(ny)]

    def hop(v):
        return lax.ppermute(v, ("c", "y"), ring)

    mine = hop(mine)
    att_other = lax.ppermute(att, "c", [(0, 1), (1, 0)])
    theirs, part = call(first_kernel, [sent, kept], (att, att_other), out_weight, weights(1), mat(2))
    theirs = hop(theirs)
    rest = call(
        rest_kernel, [kept] * (2 * half - 3), (att, att_other), out_weight, weights(half - 1), mat(2 * half - 3)
    )

    def add(a, b):
        return (a.astype(F32) + b).astype(BF)

    mine = hop(add(mine, part))
    for i in range(half - 2):
        theirs = hop(add(theirs, rest[2 * i + 1]))
        mine = hop(add(mine, rest[2 * i]))
    theirs = lax.ppermute(theirs, "c", [(0, 1), (1, 0)])
    total = residual.astype(F32) + rest[-1] + theirs.astype(F32) + mine.astype(F32)
    return total.astype(BF)


def solution(mesh):
    devices = mesh.devices
    ctx, ny = devices.shape
    fine = Mesh(devices.reshape(NX, ctx // (NX * NC), NC, ny), ("x", "z", "c", "y"))
    tok = ("x", "z", "c")
    placed = (P(tok, "y"), P(tok, "y"), P(tok, "y"), P(), P(tok, "y"), P("y", None))
    return jax.shard_map(local, mesh=fine, in_specs=placed, out_specs=P(tok, "y"), check_vma=False)
```

```python
import functools
import math

import jax
import jax.numpy as jnp
from jax import lax
from jax.experimental import pallas as pl
from jax.experimental.pallas import tpu as pltpu
from jax.sharding import Mesh, PartitionSpec as P

HD = 128
NX, NC = 4, 2
DOCS = 12
LOW = -1e30
GROUP = 2
FACTOR = math.log2(math.e) / math.sqrt(HD)
BF, F32 = jnp.bfloat16, jnp.float32
VMEM_BYTES = 24 << 20


def nt(a, b):
    return lax.dot_general(a, b, (((1,), (1,)), ((), ())), preferred_element_type=F32)


def dot(a, b):
    return jnp.dot(a, b, preferred_element_type=F32)


def pack_kernel(k_hbm, v_hbm, q_hbm, seg_hbm, kv_ref, q_ref, seg_ref, v_vmem, sems):
    pairs = ((v_hbm, v_vmem), (k_hbm, kv_ref.at[:, :HD]), (q_hbm, q_ref), (seg_hbm, seg_ref))
    copies = [pltpu.make_async_copy(a, b, sems.at[i]) for i, (a, b) in enumerate(pairs)]
    for copy in copies:
        copy.start()
    copies[0].wait()
    kv_ref[:, HD:] = v_vmem[...].astype(F32).T.astype(BF)
    for copy in copies[1:]:
        copy.wait()


def split3(v):
    hi = v.astype(BF).astype(F32)
    mid = (v - hi).astype(BF).astype(F32)
    return hi, mid, v - hi - mid


def attend(steps, seg_ref, own_ref, other_ref, q_refs, out_refs, acc, bias, qrows):
    nz = own_ref.shape[0] // HD
    rows = q_refs[0].shape[0]
    heads = q_refs[0].shape[1] // HD
    tile = NC * rows
    x, z, c = (lax.axis_index(n) for n in ("x", "z", "c"))
    here = (x * nz + z) * NC + c

    seg = seg_ref[...]
    below = [jnp.zeros((1, HD), F32)]
    for d in range(1, DOCS):
        below.append(jnp.sum((seg < d).astype(F32), axis=0, keepdims=True))
    below += [jnp.zeros((1, HD), F32)] * (16 - DOCS)
    below = jnp.sum(jnp.concatenate(below, axis=0), axis=1, keepdims=True).astype(jnp.int32)

    for n, s in enumerate(steps):
        exists = x + s < NX
        block = jnp.where(exists, here + s * nz * NC, here)
        seg_q = seg_ref[pl.ds(block, 1), :]
        first = jnp.zeros((1, rows), jnp.int32)
        for d in range(1, DOCS):
            first = jnp.where(seg_q >= d, below[d : d + 1, :], first)
        base = x * nz * tile
        lo = first - base
        hi0 = block * rows - base
        width = hi0 + lax.broadcasted_iota(jnp.int32, (1, rows), 1) - lo
        lo_min, lo_max = jnp.min(lo), jnp.max(lo)
        a = jnp.clip(lo_min // tile, 0, nz)
        b = jnp.clip((hi0 + rows - 1) // tile + 1, 0, nz)
        a = jnp.where(exists, a, 0)
        b = jnp.where(exists, jnp.maximum(a, b), 0)
        full_a = jnp.clip((lo_max + tile - 1) // tile, a, b)
        full_b = jnp.clip((hi0 + 1) // tile, full_a, b)
        acc[...] = jnp.zeros_like(acc)

        for g in range(heads):
            qrows[g * rows : (g + 1) * rows, :] = q_refs[n][:, g * HD : (g + 1) * HD]
        kv = (own_ref, other_ref)
        joint = 2
        chunks = [slice(i * joint * rows, (i + 1) * joint * rows) for i in range(heads // joint)]

        def place(t):
            return pl.ds(pl.multiple_of(t * rows, rows), rows)

        def advance(ts, state, masked):
            scores = [
                [nt(ref[place(t), :HD], qrows[at, :]) for t in ts for ref in kv] for at in chunks
            ]
            vals = jnp.concatenate([ref[place(t), HD:] for t in ts for ref in kv], axis=1)
            new = []
            for at, tiles, (m, l) in zip(chunks, scores, state):
                if masked:
                    tiles = [v + jnp.concatenate([bias[i]] * joint, axis=1) for i, v in enumerate(tiles)]
                top = functools.reduce(jnp.maximum, tiles)
                m_new = jnp.maximum(m, jnp.max(top, axis=0, keepdims=True))
                fade = jnp.exp2((m - m_new) * FACTOR)
                p = [jnp.exp2((v - m_new) * FACTOR) for v in tiles]
                l = l * fade + jnp.sum(functools.reduce(jnp.add, p), axis=0, keepdims=True)
                weights = jnp.concatenate([v.astype(BF) for v in p], axis=0)
                acc[:, at] = acc[:, at] * fade + dot(vals, weights)
                new.append((m_new, l))
            return tuple(new)

        def edge(t, state):
            for i, core in enumerate((c, 1 - c)):
                at = (t * NC + core) * rows
                off = lax.broadcasted_iota(jnp.int32, (rows, rows), 0) + (at - lo)
                bias[i] = jnp.where((off >= 0) & (off <= width), 0.0, -jnp.inf)
            return advance([t], state, True)

        def inner(i, state):
            t = full_a + GROUP * i
            return advance([t + j for j in range(GROUP)], state, False)

        none = jnp.full((1, joint * rows), LOW, F32), jnp.zeros((1, joint * rows), F32)
        state = (none,) * len(chunks)
        state = lax.fori_loop(a, full_a, edge, state)
        groups = (full_b - full_a) // GROUP
        state = lax.fori_loop(0, groups, inner, state)
        state = lax.fori_loop(full_a + GROUP * groups, b, edge, state)

        for at, (m, l) in zip(chunks, state):
            if s == 0:
                o_ref, stat_ref = out_refs
                o_ref[:, at] = acc[:, at]
                stat_ref[0:1, at] = m
                stat_ref[1:2, at] = l
            else:
                out = out_refs[n]
                out[:HD, at] = acc[:, at].astype(BF)
                line = lax.broadcasted_iota(jnp.int32, (16, m.shape[1]), 0)
                stat = jnp.zeros(line.shape, F32)
                for i, v in enumerate((*split3(m), *split3(l))):
                    stat = jnp.where(line == i, v, stat)
                out[HD:, at] = stat.astype(BF)


def far_kernel(seg, own, other, q1, q2, out1, out2, *scratch):
    attend((1, 2), seg, own, other, (q1, q2), (out1, out2), *scratch)


def near_kernel(seg, own, other, q, w_hbm, o, stat, w_ref, sem, *scratch):
    copy = pltpu.make_async_copy(w_hbm, w_ref, sem)
    copy.start()
    attend((0,), seg, own, other, (q,), (o, stat), *scratch)
    copy.wait()


def columns(w_ref, k, cols):
    ny = lax.axis_size("y")
    to = lax.rem(lax.axis_index("y") + k * (1 - 2 * lax.axis_index("c")) + ny, ny)
    return w_ref[:, pl.ds(pl.multiple_of(to * cols, cols), cols)]


def products(att, w_ref, outs, steps):
    for out, k in zip(outs, steps):
        out[...] = dot(att, columns(w_ref, k, out.shape[1])).astype(out.dtype)


def merge_kernel(o_ref, stat_ref, pay1, pay2, w_ref, att_ref, *outs):
    heads = att_ref.shape[1] // HD
    x = lax.axis_index("x")
    for g in range(heads):
        at = slice(g * HD, (g + 1) * HD)
        parts = [(stat_ref[0:1, at], stat_ref[1:2, at], o_ref[:, at])]
        for s, pay in ((1, pay1), (2, pay2)):
            stat = pay[HD:, at].astype(F32)
            m = stat[0:1] + stat[1:2] + stat[2:3]
            l = stat[3:4] + stat[4:5] + stat[5:6]
            parts.append((jnp.where(x >= s, m, LOW), l, pay[:HD, at].astype(F32)))
        top = jnp.maximum(jnp.maximum(parts[0][0], parts[1][0]), parts[2][0])
        total, summed = 0.0, 0.0
        for m, l, o in parts:
            share = jnp.exp2((m - top) * FACTOR)
            total = total + l * share
            summed = summed + o * share
        att_ref[:, at] = (summed / total).T.astype(BF)
    products(att_ref[...], w_ref, outs, (4, 3))


def mine_kernel(att, w_ref, *outs):
    products(att[...], w_ref, outs, (2, 1, 0))


def theirs_kernel(att, w_ref, *outs):
    products(att[...], w_ref, outs, (3, 2, 1))


def vmem(n):
    return [pl.BlockSpec(memory_space=pltpu.VMEM)] * n


def call(kernel, out_shape, args, hbm=(), scratch=(), cost=None):
    placed = [pltpu.with_memory_space_constraint(a, pltpu.VMEM) for a in args]
    placed += [pltpu.with_memory_space_constraint(a, pltpu.HBM) for a in hbm]
    return pl.pallas_call(
        kernel,
        out_shape=tuple(out_shape),
        in_specs=vmem(len(args)) + [pl.BlockSpec(memory_space=pltpu.HBM)] * len(hbm),
        out_specs=tuple(vmem(len(out_shape))),
        scratch_shapes=list(scratch),
        cost_estimate=cost,
        compiler_params=pltpu.CompilerParams(vmem_limit_bytes=VMEM_BYTES),
    )(*placed)


def local(queries, keys, values, segments, residual, out_weight):
    rows = queries.shape[0]
    width = queries.shape[1]
    nq = width // HD * rows
    nz, ny = lax.axis_size("z"), lax.axis_size("y")
    cols = out_weight.shape[1] // ny
    assert ny == 8
    sds = jax.ShapeDtypeStruct
    seg = segments.reshape(-1, HD)

    q1 = lax.ppermute(queries, "x", [(i + 1, i) for i in range(NX - 1)])
    q2 = lax.ppermute(queries, "x", [(i + 2, i) for i in range(NX - 2)])
    kv, near_q, seg = call(
        pack_kernel,
        [sds((rows, 2 * HD), BF), sds((rows, width), BF), sds(seg.shape, seg.dtype)],
        (),
        (keys, values, queries, seg),
        [pltpu.VMEM((rows, HD), BF), pltpu.SemaphoreType.DMA((4,))],
    )
    own = lax.all_gather(kv, "z", axis=0, tiled=True)
    other = lax.ppermute(own, "c", [(0, 1), (1, 0)])

    scratch = [pltpu.VMEM((HD, nq), F32), pltpu.VMEM((2, rows, rows), F32), pltpu.VMEM((nq, HD), BF)]
    work = 4 * nq * nz * NC * rows * HD // 2
    cost = pl.CostEstimate(flops=work, bytes_accessed=nz * rows * HD * 8, transcendentals=work // 512)
    pay = sds((HD + 16, nq), BF)
    pay1, pay2 = call(far_kernel, [pay, pay], (seg, own, other, q1, q2), (), scratch, cost)
    back1 = lax.ppermute(pay1, "x", [(i, i + 1) for i in range(NX - 1)])
    back2 = lax.ppermute(pay2, "x", [(i, i + 2) for i in range(NX - 2)])
    o, stat, w = call(
        near_kernel,
        [sds((HD, nq), F32), sds((8, nq), F32), sds(out_weight.shape, BF)],
        (seg, own, other, near_q),
        (out_weight,),
        [pltpu.SemaphoreType.DMA, *scratch],
        cost,
    )

    def mat(n):
        return pl.CostEstimate(
            flops=2 * n * rows * width * cols, bytes_accessed=n * cols * width, transcendentals=0
        )

    sent, kept = sds((rows, cols), BF), sds((rows, cols), F32)
    att, p4, p3 = call(
        merge_kernel, [sds((rows, width), BF), sent, sent], (o, stat, back1, back2, w), cost=mat(2)
    )

    def hop(v, k=1):
        perm = [(i, (i + k) % ny) for i in range(ny)] + [(ny + i, ny + (i - k) % ny) for i in range(ny)]
        return lax.ppermute(v, ("c", "y"), perm)

    def trade(v):
        return lax.ppermute(v, "c", [(0, 1), (1, 0)])

    def add(*terms):
        return functools.reduce(jnp.add, [t.astype(F32) for t in terms]).astype(BF)

    far_mine, near_mine = hop(p4, 2), hop(p3)
    att_other = trade(att)
    p2, p1, p0 = call(mine_kernel, [kept] * 3, (att, w), cost=mat(3))
    t3, t2, t1 = call(theirs_kernel, [sent, sent, kept], (att_other, w), cost=mat(3))
    far_theirs, near_theirs = hop(t3, 2), hop(t2)
    mine = hop(add(far_mine, near_mine, p2))
    theirs = hop(add(far_theirs, near_theirs, t1))
    mine = hop(add(mine, p1))
    theirs = trade(theirs)
    return add(residual, p0, theirs, mine)


def solution(mesh):
    devices = mesh.devices
    ctx, ny = devices.shape
    fine = Mesh(devices.reshape(NX, ctx // (NX * NC), NC, ny), ("x", "z", "c", "y"))
    tok = ("x", "z", "c")
    placed = (P(tok, "y"), P(tok, "y"), P(tok, "y"), P(), P(tok, "y"), P("y", None))
    return jax.shard_map(local, mesh=fine, in_specs=placed, out_specs=P(tok, "y"), check_vma=False)
```

```python
import functools
import math

import jax
import jax.numpy as jnp
from jax import lax
from jax.experimental import pallas as pl
from jax.experimental.pallas import tpu as pltpu
from jax.sharding import Mesh, PartitionSpec as P

HD = 128
NX, NC = 4, 2
DOCS = 12
LOW = -1e30
GROUPS = (4, 2, 1)
FACTOR = math.log2(math.e) / math.sqrt(HD)
BF, F32 = jnp.bfloat16, jnp.float32
VMEM_BYTES = 24 << 20


def nt(a, b):
    return lax.dot_general(a, b, (((1,), (1,)), ((), ())), preferred_element_type=F32)


def dot(a, b):
    return jnp.dot(a, b, preferred_element_type=F32)


def pack_kernel(k_hbm, v_hbm, q_hbm, seg_hbm, kv_ref, q_ref, seg_ref, v_vmem, sems):
    pairs = ((v_hbm, v_vmem), (k_hbm, kv_ref.at[:, :HD]), (q_hbm, q_ref), (seg_hbm, seg_ref))
    copies = [pltpu.make_async_copy(a, b, sems.at[i]) for i, (a, b) in enumerate(pairs)]
    for copy in copies:
        copy.start()
    copies[0].wait()
    kv_ref[:, HD:] = v_vmem[...].astype(F32).T.astype(BF)
    for copy in copies[1:]:
        copy.wait()


def split3(v):
    hi = v.astype(BF).astype(F32)
    mid = (v - hi).astype(BF).astype(F32)
    return hi, mid, v - hi - mid


def attend(steps, seg_ref, own_ref, other_ref, q_refs, out_refs, acc, bias, qrows):
    nz = own_ref.shape[0] // HD
    rows = q_refs[0].shape[0]
    heads = q_refs[0].shape[1] // HD
    tile = NC * rows
    x, z, c = (lax.axis_index(n) for n in ("x", "z", "c"))
    here = (x * nz + z) * NC + c

    seg = seg_ref[...]
    below = [jnp.zeros((1, HD), F32)]
    for d in range(1, DOCS):
        below.append(jnp.sum((seg < d).astype(F32), axis=0, keepdims=True))
    below += [jnp.zeros((1, HD), F32)] * (16 - DOCS)
    below = jnp.sum(jnp.concatenate(below, axis=0), axis=1, keepdims=True).astype(jnp.int32)

    for n, s in enumerate(steps):
        exists = x + s < NX
        block = jnp.where(exists, here + s * nz * NC, here)
        seg_q = seg_ref[pl.ds(block, 1), :]
        first = jnp.zeros((1, rows), jnp.int32)
        for d in range(1, DOCS):
            first = jnp.where(seg_q >= d, below[d : d + 1, :], first)
        base = x * nz * tile
        lo = first - base
        hi0 = block * rows - base
        width = hi0 + lax.broadcasted_iota(jnp.int32, (1, rows), 1) - lo
        lo_min, lo_max = jnp.min(lo), jnp.max(lo)
        a = jnp.clip(lo_min // tile, 0, nz)
        b = jnp.clip((hi0 + rows - 1) // tile + 1, 0, nz)
        a = jnp.where(exists, a, 0)
        b = jnp.where(exists, jnp.maximum(a, b), 0)
        full_a = jnp.clip((lo_max + tile - 1) // tile, a, b)
        full_b = jnp.clip((hi0 + 1) // tile, full_a, b)
        acc[...] = jnp.zeros_like(acc)

        for g in range(heads):
            qrows[g * rows : (g + 1) * rows, :] = q_refs[n][:, g * HD : (g + 1) * HD]
        kv = (own_ref, other_ref)
        joint = 2
        chunks = [slice(i * joint * rows, (i + 1) * joint * rows) for i in range(heads // joint)]

        def place(t):
            return pl.ds(pl.multiple_of(t * rows, rows), rows)

        def advance(ts, state, masked):
            scores = [
                [nt(ref[place(t), :HD], qrows[at, :]) for t in ts for ref in kv] for at in chunks
            ]
            vals = jnp.concatenate([ref[place(t), HD:] for t in ts for ref in kv], axis=1)
            new = []
            for at, tiles, (m, l) in zip(chunks, scores, state):
                if masked:
                    tiles = [v + jnp.concatenate([bias[i]] * joint, axis=1) for i, v in enumerate(tiles)]
                top = functools.reduce(jnp.maximum, tiles)
                m_new = jnp.maximum(m, jnp.max(top, axis=0, keepdims=True))
                fade = jnp.exp2((m - m_new) * FACTOR)
                p = [jnp.exp2((v - m_new) * FACTOR) for v in tiles]
                l = l * fade + jnp.sum(functools.reduce(jnp.add, p), axis=0, keepdims=True)
                weights = jnp.concatenate([v.astype(BF) for v in p], axis=0)
                acc[:, at] = acc[:, at] * fade + dot(vals, weights)
                new.append((m_new, l))
            return tuple(new)

        def edge(t, state):
            for i, core in enumerate((c, 1 - c)):
                at = (t * NC + core) * rows
                off = lax.broadcasted_iota(jnp.int32, (rows, rows), 0) + (at - lo)
                bias[i] = jnp.where((off >= 0) & (off <= width), 0.0, -jnp.inf)
            return advance([t], state, True)

        def inner(start, group, i, state):
            return advance([start + group * i + j for j in range(group)], state, False)

        none = jnp.full((1, joint * rows), LOW, F32), jnp.zeros((1, joint * rows), F32)
        state = (none,) * len(chunks)
        state = lax.fori_loop(a, full_a, edge, state)
        done = full_a
        for group in GROUPS:
            count = (full_b - done) // group
            state = lax.fori_loop(0, count, functools.partial(inner, done, group), state)
            done = done + group * count
        state = lax.fori_loop(full_b, b, edge, state)

        for at, (m, l) in zip(chunks, state):
            if s == 0:
                o_ref, stat_ref = out_refs
                o_ref[:, at] = acc[:, at]
                stat_ref[0:1, at] = m
                stat_ref[1:2, at] = l
            else:
                out = out_refs[n]
                out[:HD, at] = acc[:, at].astype(BF)
                line = lax.broadcasted_iota(jnp.int32, (16, m.shape[1]), 0)
                stat = jnp.zeros(line.shape, F32)
                for i, v in enumerate((*split3(m), *split3(l))):
                    stat = jnp.where(line == i, v, stat)
                out[HD:, at] = stat.astype(BF)


def far_kernel(step, seg, own, other, q, out, *scratch):
    attend((step,), seg, own, other, (q,), (out,), *scratch)


def near_kernel(seg, own, other, q, w_hbm, o, stat, w_ref, sem, *scratch):
    copy = pltpu.make_async_copy(w_hbm, w_ref, sem)
    copy.start()
    attend((0,), seg, own, other, (q,), (o, stat), *scratch)
    copy.wait()


def columns(w_ref, k, cols):
    ny = lax.axis_size("y")
    to = lax.rem(lax.axis_index("y") + k * (1 - 2 * lax.axis_index("c")) + ny, ny)
    return w_ref[:, pl.ds(pl.multiple_of(to * cols, cols), cols)]


def products(att, w_ref, outs, steps):
    for out, k in zip(outs, steps):
        out[...] = dot(att, columns(w_ref, k, out.shape[1])).astype(out.dtype)


def merge_kernel(o_ref, stat_ref, pay1, pay2, w_ref, att_ref, *outs):
    heads = att_ref.shape[1] // HD
    x = lax.axis_index("x")
    for g in range(heads):
        at = slice(g * HD, (g + 1) * HD)
        parts = [(stat_ref[0:1, at], stat_ref[1:2, at], o_ref[:, at])]
        for s, pay in ((1, pay1), (2, pay2)):
            stat = pay[HD:, at].astype(F32)
            m = stat[0:1] + stat[1:2] + stat[2:3]
            l = stat[3:4] + stat[4:5] + stat[5:6]
            parts.append((jnp.where(x >= s, m, LOW), l, pay[:HD, at].astype(F32)))
        top = jnp.maximum(jnp.maximum(parts[0][0], parts[1][0]), parts[2][0])
        total, summed = 0.0, 0.0
        for m, l, o in parts:
            share = jnp.exp2((m - top) * FACTOR)
            total = total + l * share
            summed = summed + o * share
        att_ref[:, at] = (summed / total).T.astype(BF)
    products(att_ref[...], w_ref, outs, (4, 3))


def mine_kernel(att, w_ref, *outs):
    products(att[...], w_ref, outs, (2, 1, 0))


def theirs_kernel(att, w_ref, *outs):
    products(att[...], w_ref, outs, (3, 2, 1))


def vmem(n):
    return [pl.BlockSpec(memory_space=pltpu.VMEM)] * n


def call(kernel, out_shape, args, hbm=(), scratch=(), cost=None):
    placed = [pltpu.with_memory_space_constraint(a, pltpu.VMEM) for a in args]
    placed += [pltpu.with_memory_space_constraint(a, pltpu.HBM) for a in hbm]
    return pl.pallas_call(
        kernel,
        out_shape=tuple(out_shape),
        in_specs=vmem(len(args)) + [pl.BlockSpec(memory_space=pltpu.HBM)] * len(hbm),
        out_specs=tuple(vmem(len(out_shape))),
        scratch_shapes=list(scratch),
        cost_estimate=cost,
        compiler_params=pltpu.CompilerParams(vmem_limit_bytes=VMEM_BYTES),
    )(*placed)


def local(queries, keys, values, segments, residual, out_weight):
    rows = queries.shape[0]
    width = queries.shape[1]
    nq = width // HD * rows
    nz, ny = lax.axis_size("z"), lax.axis_size("y")
    cols = out_weight.shape[1] // ny
    assert ny == 8
    sds = jax.ShapeDtypeStruct
    seg = segments.reshape(-1, HD)

    q1 = lax.ppermute(queries, "x", [(i + 1, i) for i in range(NX - 1)])
    q2 = lax.ppermute(queries, "x", [(i + 2, i) for i in range(NX - 2)])
    kv, near_q, seg = call(
        pack_kernel,
        [sds((rows, 2 * HD), BF), sds((rows, width), BF), sds(seg.shape, seg.dtype)],
        (),
        (keys, values, queries, seg),
        [pltpu.VMEM((rows, HD), BF), pltpu.SemaphoreType.DMA((4,))],
    )
    own = lax.all_gather(kv, "z", axis=0, tiled=True)
    other = lax.ppermute(own, "c", [(0, 1), (1, 0)])

    scratch = [pltpu.VMEM((HD, nq), F32), pltpu.VMEM((2, rows, rows), F32), pltpu.VMEM((nq, HD), BF)]
    work = 4 * nq * nz * NC * rows * HD // 2
    cost = pl.CostEstimate(flops=work, bytes_accessed=nz * rows * HD * 8, transcendentals=work // 512)
    pay = sds((HD + 16, nq), BF)
    back = []
    for step, q in ((1, q1), (2, q2)):
        (out,) = call(functools.partial(far_kernel, step), [pay], (seg, own, other, q), (), scratch, cost)
        back.append(lax.ppermute(out, "x", [(i, i + step) for i in range(NX - step)]))
    o, stat, w = call(
        near_kernel,
        [sds((HD, nq), F32), sds((8, nq), F32), sds(out_weight.shape, BF)],
        (seg, own, other, near_q),
        (out_weight,),
        [pltpu.SemaphoreType.DMA, *scratch],
        cost,
    )

    def mat(n):
        return pl.CostEstimate(
            flops=2 * n * rows * width * cols, bytes_accessed=n * cols * width, transcendentals=0
        )

    sent, kept = sds((rows, cols), BF), sds((rows, cols), F32)
    att, p4, p3 = call(
        merge_kernel, [sds((rows, width), BF), sent, sent], (o, stat, *back, w), cost=mat(2)
    )

    def hop(v, k=1):
        perm = [(i, (i + k) % ny) for i in range(ny)] + [(ny + i, ny + (i - k) % ny) for i in range(ny)]
        return lax.ppermute(v, ("c", "y"), perm)

    def trade(v):
        return lax.ppermute(v, "c", [(0, 1), (1, 0)])

    def add(*terms):
        return functools.reduce(jnp.add, [t.astype(F32) for t in terms]).astype(BF)

    far_mine, near_mine = hop(p4, 2), hop(p3)
    att_other = trade(att)
    p2, p1, p0 = call(mine_kernel, [kept] * 3, (att, w), cost=mat(3))
    t3, t2, t1 = call(theirs_kernel, [sent, sent, kept], (att_other, w), cost=mat(3))
    far_theirs, near_theirs = hop(t3, 2), hop(t2)
    mine = hop(add(far_mine, near_mine, p2))
    theirs = hop(add(far_theirs, near_theirs, t1))
    mine = hop(add(mine, p1))
    theirs = trade(theirs)
    return add(residual, p0, theirs, mine)


def solution(mesh):
    devices = mesh.devices
    ctx, ny = devices.shape
    fine = Mesh(devices.reshape(NX, ctx // (NX * NC), NC, ny), ("x", "z", "c", "y"))
    tok = ("x", "z", "c")
    placed = (P(tok, "y"), P(tok, "y"), P(tok, "y"), P(), P(tok, "y"), P("y", None))
    return jax.shard_map(local, mesh=fine, in_specs=placed, out_specs=P(tok, "y"), check_vma=False)
```
